512 devices in a mesh: col: 16 (over y, x), row: 2 (over core), leaf: 16 (over z).
Axes of the slice: x: 4, y: 4, z: 16, core: 2. Of those that a mesh axis runs over, the one named last changes fastest.
Arguments:
- rhs_top: float32 [4, 16, 32, 1024], P(None, 'col', None, 'row'), may hold values from -6 to 6
- diag_inv: bfloat16 [4, 16, 1024, 1024], P(None, 'col', 'row'), may hold values from -1 to 1.25, as said below
- tile_vals: bfloat16 [4, 16, 2, 8, 4, 128, 128], P(None, 'col', None, 'row'), may hold values from -0.1875 to 0.1875
- tile_pattern: int32 [4, 16, 2, 8, 4], P(None, 'col', None, 'row'), may hold values from 0 to 7, as said below
- sub_vals: bfloat16 [16, 16, 2, 8, 4, 128, 128], P('col', 'leaf', None, 'row'), may hold values from -0.1875 to 0.1875
- sub_pattern: int32 [16, 16, 2, 8, 4], P('col', 'leaf', None, 'row'), may hold values from 0 to 7, as said below
- sub_solved: bfloat16 [16, 16, 32, 1024], P('col', 'leaf'), may hold values from -6 to 6
Outputs:
- solved: float32 [4, 16, 32, 1024], P(None, 'col', None, 'row')
- outgoing: float32 [16, 2, 32, 1024], P('col', None, None, 'row')
The draws below stay inside these ranges and needn't reach their ends.
Inputs may be any that keep to these rules, and one draw needn't show every extreme that they name: `tile_pattern`: in each row block of a panel tile the 4 column blocks are distinct. `sub_pattern`: in each row block of a subtree tile the 4 column blocks are distinct. `diag_inv`: lower triangular.
All inputs are finite; a program needn't handle non-finite values.
Results may differ from the reference program's by a relative error of at most 0.012.
Values may be sent and summed in bfloat16 or wider, within the bound.
No kernel may reach another device: no remote copies, remote signals or barrier semaphores. Data moves between devices by JAX's collectives and lax.ppermute only.
A program may use at most 64 MiB of HBM per device.

```python
import math
import jax
import jax.numpy as jnp
from jax import lax

PW = 1024
SW = 1024
BLK = 128
NRHS = 32
STEPS = 4
KB = 8
NB = 4
KBS = 8
NBS = 4
N_COL = 16
N_LEAF = 16


def draw_diag_inv(key, part):
    key_diag, key_lower = jax.random.split(key)
    diagonal = jnp.exp(jax.random.uniform(key_diag, (STEPS, N_COL, PW), jnp.float32, math.log(0.8), math.log(1.25)))
    spread = 1.04 / math.sqrt(PW)
    lower = jax.random.uniform(key_lower, (STEPS, N_COL, PW, PW), jnp.float32, -spread, spread)
    rows = lax.broadcasted_iota(jnp.int32, (PW, PW), 0)
    columns = lax.broadcasted_iota(jnp.int32, (PW, PW), 1)
    matrix = jnp.where(rows > columns, lower, 0.0) + jnp.where(rows == columns, 1.0, 0.0) * diagonal[..., None]
    return matrix.astype(jnp.bfloat16)


def distinct_blocks(key, lead, total, keep):
    scores = jax.random.randint(key, lead + (total,), 0, 1 << 20) * total
    scores = scores + lax.broadcasted_iota(jnp.int32, lead + (total,), len(lead))
    order = jnp.argsort(scores, axis=-1)
    return order[..., :keep].astype(jnp.int32)


def draw_tile_pattern(key, part):
    return distinct_blocks(jax.random.fold_in(key, 11), (STEPS, N_COL, 2, KB), KB, NB)


def draw_sub_pattern(key, part):
    return distinct_blocks(jax.random.fold_in(key, 23), (N_COL, N_LEAF, 2, KB), KBS, NBS)


def levels(own_key, dims, shards, low, largest):
    loudness = 1.0
    for dim, parts in shards:
        steps = jax.random.uniform(jax.random.fold_in(jax.random.fold_in(own_key, 6), dim), (parts,), jnp.float32, low / len(shards), largest / len(shards))
        loudness = loudness * jnp.repeat(jnp.exp(steps), dims[dim] // parts).reshape((-1,) + (1,) * (len(dims) - 1 - dim))
    return loudness


def scatter_about(rng, dims, scale, limit, shards=(), dtype=jnp.bfloat16):
    drawn = jax.random.normal(rng, dims, jnp.float32) * scale
    if len(shards) > 0:
        drawn = levels(rng, dims, shards, -0.22, 0.18) * drawn
    return jnp.clip(drawn, min=-limit, max=limit).astype(dtype)


def setup_inputs(seed: int = 0) -> dict:
    seeds = jax.random.split(jax.random.key(seed), 8)
    return {
        "rhs_top": scatter_about(seeds[0], (STEPS, N_COL, NRHS, PW), 1.0, 6.0, ((1, 16), (3, 2)), jnp.float32),
        "diag_inv": draw_diag_inv(jax.random.fold_in(seeds[7], 71), 0),
        "tile_vals": scatter_about(seeds[2], (STEPS, N_COL, 2, KB, NB, BLK, BLK), PW ** -0.5, 0.1875, ((1, 16), (3, 2))),
        "tile_pattern": draw_tile_pattern(jax.random.fold_in(seeds[7], 71), 0),
        "sub_vals": scatter_about(seeds[4], (N_COL, N_LEAF, 2, KB, NBS, BLK, BLK), SW ** -0.5, 0.1875, ((0, 16), (1, 16), (3, 2))),
        "sub_pattern": draw_sub_pattern(jax.random.fold_in(seeds[7], 71), 0),
        "sub_solved": scatter_about(seeds[6], (N_COL, N_LEAF, NRHS, SW), 1.0, 6.0, ((0, 16), (1, 16))),
    }


def blocked_product(vectors, values, pattern):
    count, nrows, width = vectors.shape
    blocks = vectors.reshape(count, nrows, width // BLK, BLK).transpose(0, 2, 1, 3)
    chosen = jax.vmap(lambda blk_rows, pat: blk_rows[pat])(blocks, pattern)
    result = jnp.einsum("nhbkri,nhbkij->nhrbj", chosen.astype(jnp.float32), values.astype(jnp.float32))
    return result.reshape(count, 2, nrows, PW)


def reference(rhs_top, diag_inv, tile_vals, tile_pattern, sub_vals, sub_pattern, sub_solved):
    flat_vals = sub_vals.reshape((N_COL * N_LEAF,) + sub_vals.shape[2:])
    flat_pattern = sub_pattern.reshape((N_COL * N_LEAF,) + sub_pattern.shape[2:])
    flat_solved = sub_solved.reshape((N_COL * N_LEAF,) + sub_solved.shape[2:])
    partial_value = blocked_product(flat_solved, flat_vals, flat_pattern)
    carry = jnp.sum(partial_value.reshape(N_COL, N_LEAF, 2, NRHS, PW), axis=1)
    outputs = []
    for level in range(STEPS):
        rhs = rhs_top[level] - carry[:, 0]
        rhs_b = rhs.astype(jnp.bfloat16)
        solved = jnp.einsum("cri,cji->crj", rhs_b.astype(jnp.float32), diag_inv[level].astype(jnp.float32))
        outputs.append(solved)
        solved_b = solved.astype(jnp.bfloat16)
        update = blocked_product(solved_b, tile_vals[level], tile_pattern[level])
        sent = jnp.stack([update[:, 0] + carry[:, 1], update[:, 1]], axis=1)
        carry = jnp.roll(sent, 1, axis=0)
    return jnp.stack(outputs, axis=0), carry
```

```python
import functools

import jax
import jax.numpy as jnp
from jax import lax
from jax.experimental import pallas as pl
from jax.experimental.pallas import tpu as pltpu
from jax.sharding import PartitionSpec as P


STEPS = 4
BLK = 128
NB = 4
HALF = NB * BLK
NRHS = 32
NEAR = 4
RING = 4
LIMIT = 44
EDGE = 48
F32 = jnp.float32
BF16 = jnp.bfloat16

vmem = pl.BlockSpec(memory_space=pltpu.VMEM)
smem = pl.BlockSpec(memory_space=pltpu.SMEM)
hbm = pl.BlockSpec(memory_space=pltpu.HBM)


def dot(lhs, rhs, side):
    return lax.dot_general(lhs, rhs, (((1,), (side,)), ((), ())), preferred_element_type=F32)


def subtree_kernel(pat, solved, vals, out):
    for h in range(2):
        for b in range(NB):
            cols = [pl.multiple_of(pat[0, 0, h, b, k] * BLK, BLK) for k in range(NB)]
            lhs = jnp.concatenate([solved[:, pl.ds(c, BLK)] for c in cols], axis=1)
            part = dot(lhs, vals[h, b], 0).astype(BF16)
            for copy in range(out.shape[0]):
                out[copy, h, :, b * BLK : (b + 1) * BLK] = part


def merge_kernel(parts, out):
    total = parts[0].astype(F32)
    for i in range(1, parts.shape[0]):
        total = total + parts[i].astype(F32)
    total = total.astype(out.dtype)
    for copy in range(out.shape[0]):
        out[copy] = total


def panel_copies(level, own, other, tiles, inverse, held, sems):
    me = lax.axis_index("row")
    waits = []
    for part in range(4):
        lo, width = (part % 2) * 256, (part + 1) * 256
        dst = inverse.at[part * 256 : (part + 1) * 256, :width]
        mine, theirs = (
            pltpu.make_async_copy(src.at[level, lo : lo + 256, :width], dst, sems.at[part])
            for src in (own, other)
        )
        pl.when(me == part // 2)(mine.start)
        pl.when(me != part // 2)(theirs.start)
        waits.append(mine.wait)
    last = pltpu.make_async_copy(tiles.at[level], held, sems.at[4])
    last.start()
    return waits + [last.wait]


def level_kernel(level, front, whole, carry, pat, own, other, tiles, *refs):
    refs = list(refs)
    passed = None if front else (refs.pop(0), refs.pop(0))
    here = None if level == 0 else (refs.pop(0), refs.pop(0))
    solved, send = refs.pop(0), refs.pop(0)
    ahead = (refs.pop(0), refs.pop(0)) if level < STEPS - 1 else None
    blocks, picks, sems, ahead_sems = refs[:4]
    behind = lax.rem(lax.axis_index("col"), RING) == 0

    def work():
        inverse, held = here or (refs[4], refs[5])
        pattern = pltpu.make_async_copy(pat, picks, sems.at[5])
        pattern.start()
        waits = [lambda: None] * 5
        if here is None:
            waits = panel_copies(level, own, other, tiles, inverse, held, sems)
        later = panel_copies(level + 1, own, other, tiles, *ahead, ahead_sems) if ahead else []
        me = lax.axis_index("row")
        rhs = jnp.concatenate([whole[0], whole[1]], axis=1)
        for part in range(4):
            waits[part]()
            lo, width = part * 256, (part + 1) * 256
            x = dot(rhs[:, :width], inverse[lo : lo + 256, :width], 1)
            for q in range(2):
                blocks[part * 2 + q] = x[:, q * BLK : (q + 1) * BLK].astype(BF16)

            @pl.when(me == part // 2)
            def _():
                solved[:, (part % 2) * 256 : (part % 2) * 256 + 256] = x

        pattern.wait()
        waits[4]()
        for h in range(2):
            for b in range(NB):
                base = ((level * 2 + h) * NB + b) * NB
                lhs = jnp.concatenate([blocks[picks[base + k]] for k in range(NB)], axis=1)
                out = dot(lhs, held[h, b], 0)
                at = (slice(None), slice(b * BLK, (b + 1) * BLK))
                if h == 0:
                    out = out + carry[(1, *at)].astype(F32)
                send[(h, *at)] = out.astype(BF16)
        for wait in later:
            wait()

    if front:
        pl.when(jnp.logical_not(behind))(work)
    else:
        pl.when(behind)(work)

        @pl.when(jnp.logical_not(behind))
        def _():
            solved[...] = passed[0][...]
            send[...] = passed[1][...]


def call(kernel, out, in_specs, scratch=(), flops=0, moved=0, limit=None):
    many = isinstance(out, (tuple, list))
    return pl.pallas_call(
        kernel,
        out_shape=out,
        in_specs=in_specs,
        out_specs=[vmem] * len(out) if many else vmem,
        scratch_shapes=list(scratch),
        compiler_params=pltpu.CompilerParams(vmem_limit_bytes=limit),
        cost_estimate=pl.CostEstimate(flops=flops, bytes_accessed=moved, transcendentals=0),
    )


def exchange(parts, groups):
    return lax.all_to_all(
        parts, "leaf", split_axis=0, concat_axis=0, tiled=True, axis_index_groups=groups
    )


def chain(rhs_top, diag_inv, tile_vals, tile_pattern, sub_vals, sub_pattern, sub_solved):
    leaves = lax.axis_size("leaf")
    cols = lax.axis_size("col")
    state = (2, NRHS, HALF)
    near = [list(range(i, i + NEAR)) for i in range(0, leaves, NEAR)]
    far = [list(range(i, leaves, NEAR)) for i in range(NEAR)]
    copies = call(
        subtree_kernel,
        jax.ShapeDtypeStruct((len(near[0]), *state), BF16),
        [smem, vmem, vmem],
        flops=2 * 32 * 32 * 128 * 128,
        moved=1 << 20,
    )(sub_pattern, sub_solved[0, 0], sub_vals.reshape(2, NB, NB * BLK, BLK))
    arrived = exchange(copies, near)
    copies = call(
        merge_kernel,
        jax.ShapeDtypeStruct((len(far[0]), *state), BF16),
        [vmem],
        moved=1 << 19,
        limit=8 << 20,
    )(arrived)
    arrived = exchange(copies, far)
    carry = call(
        merge_kernel,
        jax.ShapeDtypeStruct((1, *state), F32),
        [vmem],
        moved=1 << 19,
        limit=8 << 20,
    )(arrived)[0]
    own = diag_inv[:, 0]
    other = lax.ppermute(own, "row", [(0, 1), (1, 0)])
    tiles = tile_vals[:, 0].reshape(STEPS, 2, NB, NB * BLK, BLK)
    panel = (
        jax.ShapeDtypeStruct((2 * HALF, 2 * HALF), BF16),
        jax.ShapeDtypeStruct((2, NB, NB * BLK, BLK), BF16),
    )
    pattern = tile_pattern.reshape(-1)
    across = [(c, (c + 1) % cols) for c in range(RING - 1, cols, RING)]
    along = [(c, c + 1) for c in range(cols) if c % RING != RING - 1]
    solves, weights = [], {True: [], False: []}
    carries = {True: carry, False: carry}
    for level in range(STEPS):
        total = carry[0] if level == 0 else carries[True][0] + carries[False][0]
        rhs = (rhs_top[level, 0] - total.astype(F32)).astype(BF16)
        whole = lax.all_gather(rhs, "row", axis=0, tiled=False)
        last = level == STEPS - 1
        passed = []
        arrived = {}
        for front in (True, False):
            solved, send, *weights[front] = call(
                functools.partial(level_kernel, level, front),
                (
                    jax.ShapeDtypeStruct((NRHS, HALF), F32),
                    jax.ShapeDtypeStruct(state, BF16),
                    *(() if last else panel),
                ),
                [vmem, vmem, hbm, hbm, hbm, hbm] + [vmem] * len(passed + weights[front]),
                [
                    pltpu.VMEM((2 * NB, NRHS, BLK), BF16),
                    pltpu.SMEM(pattern.shape, jnp.int32),
                    pltpu.SemaphoreType.DMA((6,)),
                    pltpu.SemaphoreType.DMA((5,)),
                    *(pltpu.VMEM(p.shape, p.dtype) for p in panel if level == 0),
                ],
                flops=2 * 32 * (1 << 20),
                moved=3 << 20,
                limit=(EDGE if level in (0, STEPS - 1) else LIMIT) << 20,
            )(
                whole,
                carries[front],
                pattern,
                own,
                other,
                tiles,
                *passed,
                *weights[front],
            )
            passed = [solved, send]
            arrived[not front] = lax.ppermute(send, "col", across if front else along)
        solves.append(solved)
        carries = arrived
    outgoing = carries[True].astype(F32) + carries[False].astype(F32)
    return jnp.stack(solves, axis=0)[:, None], outgoing[None]


def solution(mesh):
    placed = (
        P(None, "col", None, "row"),
        P(None, "col", "row", None),
        P(None, "col", None, "row", None, None, None),
        P(None, "col", None, "row", None),
        P("col", "leaf", None, "row", None, None, None),
        P("col", "leaf", None, "row", None),
        P("col", "leaf", None, None),
    )
    return jax.shard_map(
        chain,
        mesh=mesh,
        in_specs=placed,
        out_specs=(P(None, "col", None, "row"), P("col", None, None, "row")),
        check_vma=False,
    )
```

```python
import functools

import jax
import jax.numpy as jnp
from jax import lax
from jax.experimental import pallas as pl
from jax.experimental.pallas import tpu as pltpu
from jax.sharding import PartitionSpec as P


STEPS = 4
BLK = 128
NB = 4
HALF = NB * BLK
NRHS = 32
NEAR = 4
RING = 4
LIMIT = 44
EDGE = 48
F32 = jnp.float32
BF16 = jnp.bfloat16

vmem = pl.BlockSpec(memory_space=pltpu.VMEM)
smem = pl.BlockSpec(memory_space=pltpu.SMEM)
hbm = pl.BlockSpec(memory_space=pltpu.HBM)


def dot(lhs, rhs, side):
    return lax.dot_general(lhs, rhs, (((1,), (side,)), ((), ())), preferred_element_type=F32)


def subtree_kernel(pat, solved, vals, out):
    for h in range(2):
        for b in range(NB):
            cols = [pl.multiple_of(pat[0, 0, h, b, k] * BLK, BLK) for k in range(NB)]
            lhs = jnp.concatenate([solved[:, pl.ds(c, BLK)] for c in cols], axis=1)
            part = dot(lhs, vals[h, b], 0).astype(BF16)
            for copy in range(out.shape[0]):
                out[copy, h, :, b * BLK : (b + 1) * BLK] = part


def merge_kernel(parts, out):
    total = parts[0].astype(F32)
    for i in range(1, parts.shape[0]):
        total = total + parts[i].astype(F32)
    total = total.astype(out.dtype)
    for copy in range(out.shape[0]):
        out[copy] = total


def sum_kernel(*refs):
    *parts, out = refs
    total = parts[0][...].astype(F32)
    for part in parts[1:]:
        total = total + part[...].astype(F32)
    out[...] = total


def panel_copies(level, own, other, tiles, inverse, held, sems):
    me = lax.axis_index("row")
    waits = []
    for part in range(4):
        lo, width = (part % 2) * 256, (part + 1) * 256
        dst = inverse.at[part * 256 : (part + 1) * 256, :width]
        mine, theirs = (
            pltpu.make_async_copy(src.at[level, lo : lo + 256, :width], dst, sems.at[part])
            for src in (own, other)
        )
        pl.when(me == part // 2)(mine.start)
        pl.when(me != part // 2)(theirs.start)
        waits.append(mine.wait)
    last = pltpu.make_async_copy(tiles.at[level], held, sems.at[4])
    last.start()
    return waits + [last.wait]


def load_kernel(own, other, tiles, inverse, held, sems):
    for wait in panel_copies(0, own, other, tiles, inverse, held, sems):
        wait()


def level_kernel(level, front, whole, carry, late, pat, own, other, tiles, *refs):
    refs = list(refs)
    passed = None if front else (refs.pop(0), refs.pop(0))
    inverse, held = refs.pop(0), refs.pop(0)
    solved, send = refs.pop(0), refs.pop(0)
    ahead = (refs.pop(0), refs.pop(0)) if level < STEPS - 1 else None
    blocks, picks, sem, ahead_sems = refs
    behind = lax.rem(lax.axis_index("col"), RING) == 0

    def work():
        pattern = pltpu.make_async_copy(pat, picks, sem)
        pattern.start()
        later = panel_copies(level + 1, own, other, tiles, *ahead, ahead_sems) if ahead else []
        me = lax.axis_index("row")
        rhs = jnp.concatenate([whole[0], whole[1]], axis=1)
        for part in range(4):
            lo, width = part * 256, (part + 1) * 256
            x = dot(rhs[:, :width], inverse[lo : lo + 256, :width], 1)
            for q in range(2):
                blocks[part * 2 + q] = x[:, q * BLK : (q + 1) * BLK].astype(BF16)

            @pl.when(me == part // 2)
            def _():
                solved[:, (part % 2) * 256 : (part % 2) * 256 + 256] = x

        pattern.wait()
        for h in range(2):
            for b in range(NB):
                base = ((level * 2 + h) * NB + b) * NB
                lhs = jnp.concatenate([blocks[picks[base + k]] for k in range(NB)], axis=1)
                out = dot(lhs, held[h, b], 0)
                at = (slice(None), slice(b * BLK, (b + 1) * BLK))
                if h == 0:
                    out = out + carry[(1, *at)].astype(F32)
                    if level > 0:
                        out = out + late[(1, *at)].astype(F32)
                send[(h, *at)] = out.astype(BF16)
        for wait in later:
            wait()

    if front:
        pl.when(jnp.logical_not(behind))(work)
    else:
        pl.when(behind)(work)

        @pl.when(jnp.logical_not(behind))
        def _():
            solved[...] = passed[0][...]
            send[...] = passed[1][...]


def call(kernel, out, in_specs, scratch=(), flops=0, moved=0, limit=None):
    many = isinstance(out, (tuple, list))
    return pl.pallas_call(
        kernel,
        out_shape=out,
        in_specs=in_specs,
        out_specs=[vmem] * len(out) if many else vmem,
        scratch_shapes=list(scratch),
        compiler_params=pltpu.CompilerParams(vmem_limit_bytes=limit),
        cost_estimate=pl.CostEstimate(flops=flops, bytes_accessed=moved, transcendentals=0),
    )


def exchange(parts, groups):
    return lax.all_to_all(
        parts, "leaf", split_axis=0, concat_axis=0, tiled=True, axis_index_groups=groups
    )


def chain(rhs_top, diag_inv, tile_vals, tile_pattern, sub_vals, sub_pattern, sub_solved):
    leaves = lax.axis_size("leaf")
    cols = lax.axis_size("col")
    state = (2, NRHS, HALF)
    near = [list(range(i, i + NEAR)) for i in range(0, leaves, NEAR)]
    copies = call(
        subtree_kernel,
        jax.ShapeDtypeStruct((len(near[0]), *state), BF16),
        [smem, vmem, vmem],
        flops=2 * 32 * 32 * 128 * 128,
        moved=1 << 20,
    )(sub_pattern, sub_solved[0, 0], sub_vals.reshape(2, NB, NB * BLK, BLK))
    arrived = exchange(copies, near)
    part = call(
        merge_kernel,
        jax.ShapeDtypeStruct((1, *state), BF16),
        [vmem],
        moved=1 << 19,
        limit=8 << 20,
    )(arrived)
    parts = [part]
    for d in (2 * NEAR, NEAR, 3 * NEAR):
        route = [(i, (i + d) % leaves) for i in range(leaves)]
        parts.append(lax.ppermute(part, "leaf", route))
    carry = call(
        sum_kernel,
        jax.ShapeDtypeStruct((1, *state), F32),
        [vmem] * len(parts),
        moved=1 << 19,
        limit=8 << 20,
    )(*parts)[0]
    own = diag_inv[:, 0]
    other = lax.ppermute(own, "row", [(0, 1), (1, 0)])
    tiles = tile_vals[:, 0].reshape(STEPS, 2, NB, NB * BLK, BLK)
    panel = (
        jax.ShapeDtypeStruct((2 * HALF, 2 * HALF), BF16),
        jax.ShapeDtypeStruct((2, NB, NB * BLK, BLK), BF16),
    )
    pattern = tile_pattern.reshape(-1)
    moves = {
        True: [(c, (c + 1) % cols) for c in range(cols) if c % RING],
        False: [(c, c + 1) for c in range(0, cols, RING)],
    }
    loaded = call(
        load_kernel,
        panel,
        [hbm, hbm, hbm],
        [pltpu.SemaphoreType.DMA((5,))],
        moved=3 << 20,
        limit=EDGE << 20,
    )(own, other, tiles)
    solves, weights = [], {True: list(loaded), False: list(loaded)}
    carries = {True: carry, False: carry}
    for level in range(STEPS):
        total = carry[0] if level == 0 else carries[True][0] + carries[False][0]
        rhs = (rhs_top[level, 0] - total.astype(F32)).astype(BF16)
        whole = lax.all_gather(rhs, "row", axis=0, tiled=False)
        last = level == STEPS - 1
        passed = []
        arrived = {}
        for front in (True, False):
            solved, send, *weights[front] = call(
                functools.partial(level_kernel, level, front),
                (
                    jax.ShapeDtypeStruct((NRHS, HALF), F32),
                    jax.ShapeDtypeStruct(state, BF16),
                    *(() if last else panel),
                ),
                [vmem, vmem, vmem, hbm, hbm, hbm, hbm] + [vmem] * len(passed + weights[front]),
                [
                    pltpu.VMEM((2 * NB, NRHS, BLK), BF16),
                    pltpu.SMEM(pattern.shape, jnp.int32),
                    pltpu.SemaphoreType.DMA,
                    pltpu.SemaphoreType.DMA((5,)),
                ],
                flops=2 * 32 * (1 << 20),
                moved=3 << 20,
                limit=(EDGE if last else LIMIT) << 20,
            )(
                whole,
                carries[True],
                carries[False],
                pattern,
                own,
                other,
                tiles,
                *passed,
                *weights[front],
            )
            passed = [solved, send]
            arrived[front] = lax.ppermute(send, "col", moves[front])
        solves.append(solved)
        carries = arrived
    outgoing = carries[True].astype(F32) + carries[False].astype(F32)
    return jnp.stack(solves, axis=0)[:, None], outgoing[None]


def solution(mesh):
    placed = (
        P(None, "col", None, "row"),
        P(None, "col", "row", None),
        P(None, "col", None, "row", None, None, None),
        P(None, "col", None, "row", None),
        P("col", "leaf", None, "row", None, None, None),
        P("col", "leaf", None, "row", None),
        P("col", "leaf", None, None),
    )
    return jax.shard_map(
        chain,
        mesh=mesh,
        in_specs=placed,
        out_specs=(P(None, "col", None, "row"), P("col", None, None, "row")),
        check_vma=False,
    )
```

```python
import functools

import jax
import jax.numpy as jnp
from jax import lax
from jax.experimental import pallas as pl
from jax.experimental.pallas import tpu as pltpu
from jax.sharding import PartitionSpec as P


STEPS = 4
BLK = 128
NB = 4
HALF = NB * BLK
NRHS = 32
NEAR = 4
LIMIT = 44
EDGE = 48
F32 = jnp.float32
BF16 = jnp.bfloat16

vmem = pl.BlockSpec(memory_space=pltpu.VMEM)
smem = pl.BlockSpec(memory_space=pltpu.SMEM)
hbm = pl.BlockSpec(memory_space=pltpu.HBM)


def dot(lhs, rhs, side):
    return lax.dot_general(lhs, rhs, (((1,), (side,)), ((), ())), preferred_element_type=F32)


def subtree_kernel(pat, solved, vals, out):
    for h in range(2):
        for b in range(NB):
            cols = [pl.multiple_of(pat[0, 0, h, b, k] * BLK, BLK) for k in range(NB)]
            lhs = jnp.concatenate([solved[:, pl.ds(c, BLK)] for c in cols], axis=1)
            part = dot(lhs, vals[h, b], 0).astype(BF16)
            for copy in range(out.shape[0]):
                out[copy, h, :, b * BLK : (b + 1) * BLK] = part


def merge_kernel(parts, out):
    total = parts[0].astype(F32)
    for i in range(1, parts.shape[0]):
        total = total + parts[i].astype(F32)
    total = total.astype(out.dtype)
    for copy in range(out.shape[0]):
        out[copy] = total


def sum_kernel(*refs):
    *parts, out = refs
    total = parts[0][...].astype(F32)
    for part in parts[1:]:
        total = total + part[...].astype(F32)
    out[...] = total


def panel_copies(level, own, other, tiles, inverse, held, sems):
    me = lax.axis_index("row")
    waits = []
    for part in range(4):
        lo, width = (part % 2) * 256, (part + 1) * 256
        dst = inverse.at[part * 256 : (part + 1) * 256, :width]
        mine, theirs = (
            pltpu.make_async_copy(src.at[level, lo : lo + 256, :width], dst, sems.at[part])
            for src in (own, other)
        )
        pl.when(me == part // 2)(mine.start)
        pl.when(me != part // 2)(theirs.start)
        waits.append(mine.wait)
    last = pltpu.make_async_copy(tiles.at[level], held, sems.at[4])
    last.start()
    return waits + [last.wait]


def load_kernel(own, other, tiles, inverse, held, sems):
    for wait in panel_copies(0, own, other, tiles, inverse, held, sems):
        wait()


def level_kernel(level, front, whole, carry, late, pat, own, other, tiles, *refs):
    refs = list(refs)
    passed = None if front else (refs.pop(0), refs.pop(0))
    inverse, held = refs.pop(0), refs.pop(0)
    solved, send = refs.pop(0), refs.pop(0)
    ahead = (refs.pop(0), refs.pop(0)) if level < STEPS - 1 else None
    blocks, picks, sem, ahead_sems = refs
    behind = lax.rem(lax.axis_index("col"), 2) == 0

    def work():
        pattern = pltpu.make_async_copy(pat, picks, sem)
        pattern.start()
        later = panel_copies(level + 1, own, other, tiles, *ahead, ahead_sems) if ahead else []
        me = lax.axis_index("row")
        rhs = jnp.concatenate([whole[0], whole[1]], axis=1)
        for part in range(4):
            lo, width = part * 256, (part + 1) * 256
            x = dot(rhs[:, :width], inverse[lo : lo + 256, :width], 1)
            for q in range(2):
                blocks[part * 2 + q] = x[:, q * BLK : (q + 1) * BLK].astype(BF16)

            @pl.when(me == part // 2)
            def _():
                solved[:, (part % 2) * 256 : (part % 2) * 256 + 256] = x

        pattern.wait()
        for h in range(2):
            for b in range(NB):
                base = ((level * 2 + h) * NB + b) * NB
                lhs = jnp.concatenate([blocks[picks[base + k]] for k in range(NB)], axis=1)
                out = dot(lhs, held[h, b], 0)
                at = (slice(None), slice(b * BLK, (b + 1) * BLK))
                if h == 0:
                    out = out + carry[(1, *at)].astype(F32)
                    if level > 0:
                        out = out + late[(1, *at)].astype(F32)
                send[(h, *at)] = out.astype(BF16)
        for wait in later:
            wait()

    if front:
        pl.when(jnp.logical_not(behind))(work)
    else:
        pl.when(behind)(work)

        @pl.when(jnp.logical_not(behind))
        def _():
            solved[...] = passed[0][...]
            send[...] = passed[1][...]


def call(kernel, out, in_specs, scratch=(), flops=0, moved=0, limit=None):
    many = isinstance(out, (tuple, list))
    return pl.pallas_call(
        kernel,
        out_shape=out,
        in_specs=in_specs,
        out_specs=[vmem] * len(out) if many else vmem,
        scratch_shapes=list(scratch),
        compiler_params=pltpu.CompilerParams(vmem_limit_bytes=limit),
        cost_estimate=pl.CostEstimate(flops=flops, bytes_accessed=moved, transcendentals=0),
    )


def exchange(parts, groups):
    return lax.all_to_all(
        parts, "leaf", split_axis=0, concat_axis=0, tiled=True, axis_index_groups=groups
    )


def chain(rhs_top, diag_inv, tile_vals, tile_pattern, sub_vals, sub_pattern, sub_solved):
    leaves = lax.axis_size("leaf")
    cols = lax.axis_size("col")
    state = (2, NRHS, HALF)
    near = [list(range(i, i + NEAR)) for i in range(0, leaves, NEAR)]
    copies = call(
        subtree_kernel,
        jax.ShapeDtypeStruct((len(near[0]), *state), BF16),
        [smem, vmem, vmem],
        flops=2 * 32 * 32 * 128 * 128,
        moved=1 << 20,
    )(sub_pattern, sub_solved[0, 0], sub_vals.reshape(2, NB, NB * BLK, BLK))
    arrived = exchange(copies, near)
    part = call(
        merge_kernel,
        jax.ShapeDtypeStruct((1, *state), BF16),
        [vmem],
        moved=1 << 19,
        limit=8 << 20,
    )(arrived)
    parts = [part]
    for d in (2 * NEAR, NEAR, 3 * NEAR):
        route = [(i, (i + d) % leaves) for i in range(leaves)]
        parts.append(lax.ppermute(part, "leaf", route))
    carry = call(
        sum_kernel,
        jax.ShapeDtypeStruct((1, *state), F32),
        [vmem] * len(parts),
        moved=1 << 19,
        limit=8 << 20,
    )(*parts)[0]
    own = diag_inv[:, 0]
    other = lax.ppermute(own, "row", [(0, 1), (1, 0)])
    tiles = tile_vals[:, 0].reshape(STEPS, 2, NB, NB * BLK, BLK)
    panel = (
        jax.ShapeDtypeStruct((2 * HALF, 2 * HALF), BF16),
        jax.ShapeDtypeStruct((2, NB, NB * BLK, BLK), BF16),
    )
    pattern = tile_pattern.reshape(-1)
    moves = {
        True: [(c, (c + 1) % cols) for c in range(cols) if c % 2],
        False: [(c, (c + 1) % cols) for c in range(cols) if not (c % 2)],
    }
    loaded = call(
        load_kernel,
        panel,
        [hbm, hbm, hbm],
        [pltpu.SemaphoreType.DMA((5,))],
        moved=3 << 20,
        limit=EDGE << 20,
    )(own, other, tiles)
    solves, weights = [], {True: list(loaded), False: list(loaded)}
    carries = {True: carry, False: carry}
    for level in range(STEPS):
        total = carry[0] if level == 0 else carries[True][0] + carries[False][0]
        rhs = (rhs_top[level, 0] - total.astype(F32)).astype(BF16)
        whole = lax.all_gather(rhs, "row", axis=0, tiled=False)
        last = level == STEPS - 1
        passed = []
        arrived = {}
        for front in (True, False):
            solved, send, *weights[front] = call(
                functools.partial(level_kernel, level, front),
                (
                    jax.ShapeDtypeStruct((NRHS, HALF), F32),
                    jax.ShapeDtypeStruct(state, BF16),
                    *(() if last else panel),
                ),
                [vmem, vmem, vmem, hbm, hbm, hbm, hbm] + [vmem] * len(passed + weights[front]),
                [
                    pltpu.VMEM((2 * NB, NRHS, BLK), BF16),
                    pltpu.SMEM(pattern.shape, jnp.int32),
                    pltpu.SemaphoreType.DMA,
                    pltpu.SemaphoreType.DMA((5,)),
                ],
                flops=2 * 32 * (1 << 20),
                moved=3 << 20,
                limit=(EDGE if last else LIMIT) << 20,
            )(
                whole,
                carries[True],
                carries[False],
                pattern,
                own,
                other,
                tiles,
                *passed,
                *weights[front],
            )
            passed = [solved, send]
            arrived[front] = lax.ppermute(send, "col", moves[front])
        solves.append(solved)
        carries = arrived
    outgoing = carries[True].astype(F32) + carries[False].astype(F32)
    return jnp.stack(solves, axis=0)[:, None], outgoing[None]


def solution(mesh):
    placed = (
        P(None, "col", None, "row"),
        P(None, "col", "row", None),
        P(None, "col", None, "row", None, None, None),
        P(None, "col", None, "row", None),
        P("col", "leaf", None, "row", None, None, None),
        P("col", "leaf", None, "row", None),
        P("col", "leaf", None, None),
    )
    return jax.shard_map(
        chain,
        mesh=mesh,
        in_specs=placed,
        out_specs=(P(None, "col", None, "row"), P("col", None, None, "row")),
        check_vma=False,
    )
```
